128 devices in a mesh: blk: 16 (over y_lo, z, core), leaf: 8 (over y_hi, x).
Axes of the slice: x: 4, y: 4 (y_hi: 2, y_lo: 2; y = y_hi * 2 + y_lo), z: 4, core: 2. Of those that a mesh axis runs over, the one named last changes fastest.
Arguments:
- rhs: bfloat16 [64, 262144], P(None, ('blk', 'leaf')), may hold values from -6 to 6
- basis: bfloat16 [1024, 256, 128], P(('blk', 'leaf')), may hold values from -0.375 to 0.375
- near_list: int32 [1024, 6], P(('blk', 'leaf')), may hold values from 0 to 1023, as said below
- near_block: bfloat16 [1024, 6, 256, 256], P(('blk', 'leaf')), may hold values from -0.15625 to 0.15625
- local_transfer: float32 [1024, 128, 128], P(('blk', 'leaf')), may hold values from -0.1875 to 0.1875
- cross_transfer: float32 [16, 14, 128, 128], P('blk'), may hold values from -0.375 to 0.375
- coupling_list: int32 [1024, 15, 2], P(('blk', 'leaf')), may hold values from 0 to 8, as said below
- leaf_coupling: bfloat16 [1024, 15, 2, 128, 128], P(('blk', 'leaf')), may hold values from -0.09375 to 0.09375
- root_coupling: bfloat16 [16, 15, 128, 128], P('blk'), may hold values from -0.5 to 0.5
Outputs:
- product: float32 [64, 262144], P(None, ('blk', 'leaf'))
The draws below stay inside these ranges and needn't reach their ends.
Inputs may be any that keep to these rules, and one draw needn't show every extreme that they name: near_list[g, 0] = g; every entry names a leaf of g's own subtree whose leaf node is g // 8 - 1, g // 8 or g // 8 + 1. `coupling_list`: the value 8 marks an empty slot; any other value j names the j-th leaf of the leaf node at the same position of the subtree at that offset.
All inputs are finite; a program needn't handle non-finite values.
Results may differ from the reference program's by a relative error of at most 0.0029.
Values may be sent and summed in bfloat16 or wider, within the bound.
A program may use at most 64 MiB of HBM per device.

```python
from functools import partial
import jax
import jax.numpy as jnp
from jax import lax

LEAF = 256
RANK = 128
NRHS = 64
NEAR = 6
SLOTS = 2
L_DEV = 8
GROUP = 64
NL = 1024
HOSTS = 262144
STEPS = 15
CROSS_NODES = 14
N_BLK = 16
N_LEAF = 8


def draw_near_list(key, part):
    leaf_ids = jnp.arange(NL, dtype=jnp.int32)
    position = leaf_ids % GROUP // L_DEV
    lower = jnp.where(position > 0, -L_DEV, 0).astype(jnp.int32)
    upper = jnp.where(position < GROUP // L_DEV - 1, 2 * L_DEV, L_DEV).astype(jnp.int32)
    start = leaf_ids // L_DEV * L_DEV
    offsets = jax.random.randint(key, (NL, NEAR), lower[:, None], upper[:, None], dtype=jnp.int32)
    chosen = start[:, None] + offsets
    return chosen.at[:, 0].set(leaf_ids)


def draw_coupling_list(key, part):
    values = jax.random.randint(key, (NL, STEPS, SLOTS), 0, L_DEV + 1, dtype=jnp.int32)
    return values.at[0, 0, SLOTS - 1].set(L_DEV)


def block_scale(stream_key, shape, pieces, least, high):
    def one(dim, parts):
        steps = jax.random.uniform(jax.random.fold_in(jax.random.fold_in(stream_key, 6), dim), (parts,), jnp.float32, least / len(pieces), high / len(pieces))
        return jnp.repeat(jnp.exp(steps), shape[dim] // parts).reshape((-1,) + (1,) * (len(shape) - dim - 1))

    factor_of = one(*pieces[0])
    for cut in pieces[1:]:
        factor_of = factor_of * one(*cut)
    return factor_of


def gaussian(stream_key, extent, spread, reach, cuts=(), kind=jnp.bfloat16):
    values = spread * jax.random.normal(stream_key, extent, jnp.float32)
    if cuts:
        values = values * block_scale(stream_key, extent, cuts, -0.22, 0.18)
    return jnp.clip(values, -reach, reach).astype(kind)


def setup_inputs(seed: int = 0) -> dict:
    arg_keys = jax.random.split(jax.random.key(seed), 10)
    return {
        "rhs": gaussian(arg_keys[0], (NRHS, HOSTS), 1.0, 6.0, ((1, 128),)),
        "basis": gaussian(arg_keys[1], (NL, LEAF, RANK), LEAF ** -0.5, 0.375, ((0, 128),)),
        "near_list": draw_near_list(jax.random.fold_in(arg_keys[9], 71), 0),
        "near_block": gaussian(arg_keys[3], (NL, NEAR, LEAF, LEAF), (LEAF * NEAR) ** -0.5, 0.15625, ((0, 128),)),
        "local_transfer": gaussian(arg_keys[4], (NL, RANK, RANK), (RANK * L_DEV) ** -0.5, 0.1875, ((0, 128),), jnp.float32),
        "cross_transfer": gaussian(arg_keys[5], (N_BLK, CROSS_NODES, RANK, RANK), (2 * RANK) ** -0.5, 0.375, ((0, 16),), jnp.float32),
        "coupling_list": draw_coupling_list(jax.random.fold_in(arg_keys[9], 71), 0),
        "leaf_coupling": gaussian(arg_keys[7], (NL, STEPS, SLOTS, RANK, RANK), (RANK * SLOTS * STEPS) ** -0.5, 0.09375, ((0, 128),)),
        "root_coupling": gaussian(arg_keys[8], (N_BLK, STEPS, RANK, RANK), RANK ** -0.5, 0.5, ((0, 16),)),
    }


precise = lax.Precision.HIGHEST


def climb(coeffs, transfers):
    count = coeffs.shape[0]
    while count > 1:
        matrices = transfers[count - 2:2 * count - 2]
        shares = jnp.einsum("mnr,mrq->mnq", coeffs, matrices, precision=precise)
        coeffs = shares[0::2] + shares[1::2]
        count = count // 2
    return coeffs[0]


def descend(root_value, transfers, total):
    values = root_value[None]
    count = 2
    while count <= total:
        parents = jnp.repeat(values, 2, axis=0)
        matrices = transfers[count - 2:2 * count - 2]
        values = jnp.einsum("mnq,mrq->mnr", parents, matrices, precision=precise)
        count = count * 2
    return values


def reference(rhs, basis, near_list, near_block, local_transfer, cross_transfer, coupling_list, leaf_coupling, root_coupling):
    nodes = NL // L_DEV
    columns = rhs.reshape(NRHS, NL, LEAF).transpose(1, 0, 2)
    leaf_coef = jnp.einsum("gnp,gpr->gnr", columns.astype(jnp.float32), basis.astype(jnp.float32))
    leaf_sent = leaf_coef.astype(jnp.bfloat16)
    local_mats = local_transfer.reshape(nodes, L_DEV, RANK, RANK)
    node_coef = jnp.einsum("dinr,dirq->dnq", leaf_coef.reshape(nodes, L_DEV, NRHS, RANK), local_mats, precision=precise)
    grouped = node_coef.reshape(N_BLK, N_LEAF, NRHS, RANK)
    root_coef = jax.vmap(climb)(grouped, cross_transfer)
    root_sent = root_coef.astype(jnp.bfloat16)
    leaf_ids = jnp.arange(NL, dtype=jnp.int32)
    subtree = leaf_ids // GROUP
    inside = leaf_ids % GROUP - leaf_ids % L_DEV
    blk_ids = jnp.arange(N_BLK, dtype=jnp.int32)
    leaf_far = jnp.zeros((NL, NRHS, RANK), jnp.float32)
    root_far = jnp.zeros((N_BLK, NRHS, RANK), jnp.float32)
    for offset in range(1, N_BLK):
        slot_ids = coupling_list[:, offset - 1]
        source = ((subtree - offset) % N_BLK) * GROUP + inside
        partners = (source[:, None] + jnp.minimum(slot_ids, L_DEV - 1)).astype(jnp.int32)
        valid = (slot_ids < L_DEV).astype(jnp.float32)
        picked = leaf_sent[partners].astype(jnp.float32) * valid[:, :, None, None]
        leaf_far = leaf_far + jnp.einsum("gknr,gkrq->gnq", picked, leaf_coupling[:, offset - 1].astype(jnp.float32))
        visiting = root_sent[((blk_ids - offset) % N_BLK).astype(jnp.int32)].astype(jnp.float32)
        root_far = root_far + jnp.einsum("bnr,brq->bnq", visiting, root_coupling[:, offset - 1].astype(jnp.float32))
    node_down = jax.vmap(partial(descend, total=N_LEAF))(root_far, cross_transfer).reshape(nodes, NRHS, RANK)
    down_leaf = jnp.einsum("dnq,dirq->dinr", node_down, local_mats, precision=precise).reshape(NL, NRHS, RANK)
    leaf_total = (leaf_far + down_leaf).astype(jnp.bfloat16)
    near = jnp.zeros((NL, NRHS, LEAF), jnp.float32)
    for slot in range(NEAR):
        partner_cols = columns[near_list[:, slot].astype(jnp.int32)].astype(jnp.float32)
        near = near + jnp.einsum("gnp,gpq->gnq", partner_cols, near_block[:, slot].astype(jnp.float32))
    far = jnp.einsum("gnr,gpr->gnp", leaf_total.astype(jnp.float32), basis.astype(jnp.float32))
    return (near + far).transpose(1, 0, 2).reshape(NRHS, HOSTS)
```

```python
import jax
import jax.numpy as jnp
from jax import lax
from jax.experimental import pallas as pl
from jax.experimental.pallas import tpu as pltpu
from jax.sharding import PartitionSpec as P

bf16, f32 = jnp.bfloat16, jnp.float32

N_BLK, N_LEAF = 16, 8
LEAVES, SIZE, RANK, NRHS = 8, 256, 128, 64
NEAR, SLOTS, STEPS = 6, 2, 15
ROWS = NRHS // N_LEAF

SOURCES = [
    (dy, dz, dc) for dz in (0, -1, 1, 2) for dy in (0, 1) for dc in (0, 1) if (dy, dz, dc) != (0, 0, 0)
]


def mm(a, b):
    return jnp.dot(a, b, preferred_element_type=f32)


def mm_t(a, b):
    return lax.dot_general(a, b, (((1,), (1,)), ((), ())), preferred_element_type=f32)


def split(v):
    high = v.astype(bf16)
    return high, (v - high.astype(f32)).astype(bf16)


def mm3(a_high, a_low, b_high, b_low, product=mm):
    rows = a_high.shape[0]
    both = product(jnp.concatenate([a_high, a_low], axis=0), b_high)
    return both[:rows] + both[rows:] + product(a_high, b_low)


def kernel(
    rhs, basis_hbm, near_list, near_hbm, lt_hbm, ct_hbm, coupling_list, coup_hbm, rc_hbm,
    out,
    x, basis, nlist, near_w, lt, ct, clist, coup, rc,
    own, share_buf, rs_buf, root_own, vis, rf, far_acc, prod,
    lt_h, lt_l, t_h, t_l, g_h, g_l,
    *rest,
):
    bufs = dict(zip(SOURCES, rest[: len(SOURCES)]))
    lsem, osem, barrier_unused, hs, hr, cs, cr, rs_s, rs_r, ag_s, ag_r, al_s, al_r = rest[len(SOURCES):]
    b = lax.axis_index("blk")
    l = lax.axis_index("leaf")
    core = b % 2
    z = (b // 2) % 4
    y = b // 8

    def blk_of(dy, dz, dc):
        yy = (y + dy) % 2
        zz = (z + dz + 4) % 4
        cc = (core + dc) % 2
        return yy * 8 + zz * 2 + cc

    barrier = pltpu.get_barrier_semaphore()
    for s in range(1, N_BLK):
        pl.semaphore_signal(barrier, inc=1, device_id={"blk": (b + s) % N_BLK})
    for d in range(1, N_LEAF):
        pl.semaphore_signal(barrier, inc=1, device_id={"leaf": (l + d) % N_LEAF})

    def load(src, dst, i):
        c = pltpu.make_async_copy(src, dst, lsem.at[i])
        c.start()
        return c

    x_loads = [
        load(rhs.at[:, pl.ds(g * SIZE, SIZE)], x.at[LEAVES + g], g) for g in range(LEAVES)
    ]
    basis_load = load(basis_hbm, basis, 8)
    ct_loads = [
        load(ct_hbm.at[0, 6 + l], ct.at[0], 9),
        load(ct_hbm.at[0, 2 + l // 2], ct.at[1], 10),
        load(ct_hbm.at[0, l // 4], ct.at[2], 11),
    ]
    lt_load = load(lt_hbm, lt, 12)
    nlist_load = load(near_list, nlist, 13)
    clist_load = load(coupling_list, clist, 14)
    near_loads = [load(near_hbm.at[g], near_w.at[g], 15 + g) for g in range(LEAVES)]
    rc_load = load(rc_hbm, rc, 23)
    coup_loads = [load(coup_hbm.at[g], coup.at[g], 24 + g) for g in range(LEAVES)]

    for src in SOURCES:
        bufs[src][LEAVES] = jnp.zeros((NRHS, RANK), bf16)

    for c in x_loads:
        c.wait()
    basis_load.wait()
    coef = []
    for g in range(LEAVES):
        c = mm(x[LEAVES + g], basis[g])
        coef.append(c)
        own[g] = c.astype(bf16)

    def blk_copy(src, dst, i, dy, dz, dc):
        return pltpu.make_async_remote_copy(
            src_ref=src, dst_ref=dst, send_sem=cs.at[i], recv_sem=cr.at[i],
            device_id={"blk": blk_of(dy, dz, dc)},
        )

    whole = pl.ds(0, LEAVES)
    first, second = pl.ds(0, LEAVES // 2), pl.ds(LEAVES // 2, LEAVES // 2)
    copies = {}

    def send(name, src, target, part, dy, dz, dc):
        i = len(copies)
        c = blk_copy(src.at[part], bufs[target].at[part], i, dy, dz, dc)
        copies[name] = c
        c.start()

    pl.semaphore_wait(barrier, N_BLK - 1 + N_LEAF - 1)
    send("zp", own, (0, -1, 0), whole, 0, 1, 0)
    send("zm", own, (0, 1, 0), whole, 0, -1, 0)
    send("p", own, (0, 0, 1), whole, 0, 0, 1)

    for c in ct_loads:
        c.wait()
    lt_load.wait()
    w_h, w_l = split(lt[...].reshape(LEAVES * RANK, RANK))
    lt_h[...] = w_h
    lt_l[...] = w_l
    m0, m1, m2 = [split(ct[i]) for i in range(3)]
    t = split(mm3(*m0, *m1))
    t = split(mm3(*t, *m2))
    t_h[...], t_l[...] = t
    parts = [split(c) for c in coef]
    c_h = jnp.concatenate([p[0] for p in parts], axis=1)
    c_l = jnp.concatenate([p[1] for p in parts], axis=1)
    node = mm3(c_h, c_l, lt_h[...], lt_l[...])
    share = mm3(*split(node), *t)
    share_buf[...] = share.reshape(N_LEAF, ROWS, RANK)

    rs = []
    for d in range(1, N_LEAF):
        to = (l + d) % N_LEAF
        c = pltpu.make_async_remote_copy(
            src_ref=share_buf.at[to], dst_ref=rs_buf.at[d - 1],
            send_sem=rs_s.at[d - 1], recv_sem=rs_r.at[d - 1], device_id={"leaf": to},
        )
        c.start()
        rs.append(c)
    send("y", own, (1, 0, 0), whole, 1, 0, 0)

    mine, low, high = pl.ds(LEAVES, LEAVES), pl.ds(0, LEAVES), pl.ds(2 * LEAVES, LEAVES)
    up = pltpu.make_async_remote_copy(
        src_ref=x.at[mine], dst_ref=x.at[low], send_sem=hs.at[0], recv_sem=hr.at[0],
        device_id={"leaf": (l + 1) % N_LEAF},
    )
    down = pltpu.make_async_remote_copy(
        src_ref=x.at[mine], dst_ref=x.at[high], send_sem=hs.at[1], recv_sem=hr.at[1],
        device_id={"leaf": (l + N_LEAF - 1) % N_LEAF},
    )
    has_up, has_down = l < N_LEAF - 1, l > 0
    pl.when(has_up)(up.start)
    pl.when(has_down)(down.start)

    for c in near_loads:
        c.wait()

    def near_own(g, _):
        prod[g] = mm(x[LEAVES + g], near_w[g, pl.ds(0, SIZE), :])
        return 0

    lax.fori_loop(0, LEAVES, near_own, 0, unroll=True)

    copies["zp"].wait_recv()
    send("zp_fwd", bufs[0, -1, 0], (0, 2, 0), first, 0, 1, 0)
    send("zp_p", bufs[0, -1, 0], (0, -1, 1), whole, 0, 0, 1)
    copies["zm"].wait_recv()
    send("zm_fwd", bufs[0, 1, 0], (0, 2, 0), second, 0, -1, 0)
    send("zm_p", bufs[0, 1, 0], (0, 1, 1), whole, 0, 0, 1)
    copies["y"].wait_recv()
    send("yzp", bufs[1, 0, 0], (1, -1, 0), whole, 0, 1, 0)
    send("yzm", bufs[1, 0, 0], (1, 1, 0), whole, 0, -1, 0)
    send("y_p", bufs[1, 0, 0], (1, 0, 1), whole, 0, 0, 1)

    total = share_buf[l]
    for d in range(1, N_LEAF):
        rs[d - 1].wait_recv()
        total = total + rs_buf[d - 1]
    root_own[...] = total.astype(bf16).astype(f32)
    ag = []
    for s in range(1, N_BLK):
        c = pltpu.make_async_remote_copy(
            src_ref=root_own, dst_ref=vis.at[s - 1],
            send_sem=ag_s.at[s - 1], recv_sem=ag_r.at[s - 1], device_id={"blk": (b + s) % N_BLK},
        )
        c.start()
        ag.append(c)

    clist_load.wait()
    for c in coup_loads:
        c.wait()

    def couple(sources, fresh):
        offsets = [(b - blk_of(*src) + N_BLK) % N_BLK - 1 for src in sources]

        def body(g, _):
            total = None if fresh else far_acc[g]
            for src, o in zip(sources, offsets):
                buf = bufs[src]
                lhs = jnp.concatenate([buf[clist[g, 0, o]], buf[clist[g, 1, o]]], axis=1)
                term = mm(lhs, coup[g, o])
                total = term if total is None else total + term
            far_acc[g] = total
            return 0

        lax.fori_loop(0, LEAVES, body, 0)

    copies["p"].wait_recv()
    couple([(0, 0, 1), (1, 0, 0), (0, -1, 0), (0, 1, 0)], True)

    copies["yzp"].wait_recv()
    send("yzp_fwd", bufs[1, -1, 0], (1, 2, 0), first, 0, 1, 0)
    send("yzp_p", bufs[1, -1, 0], (1, -1, 1), whole, 0, 0, 1)
    copies["yzm"].wait_recv()
    send("yzm_fwd", bufs[1, 1, 0], (1, 2, 0), second, 0, -1, 0)
    send("yzm_p", bufs[1, 1, 0], (1, 1, 1), whole, 0, 0, 1)
    copies["zp_fwd"].wait_recv()
    copies["zm_fwd"].wait_recv()
    send("z2_p", bufs[0, 2, 0], (0, 2, 1), whole, 0, 0, 1)

    rc_load.wait()
    for c in ag:
        c.wait_recv()
    lhs = jnp.concatenate([vis[s].astype(bf16) for s in range(STEPS)], axis=1)
    rows = mm(lhs, rc[...])
    rf[l] = rows
    al = []
    for d in range(1, N_LEAF):
        c = pltpu.make_async_remote_copy(
            src_ref=rf.at[l], dst_ref=rf.at[l],
            send_sem=al_s.at[d - 1], recv_sem=al_r.at[d - 1], device_id={"leaf": (l + d) % N_LEAF},
        )
        c.start()
        al.append(c)

    nlist_load.wait()
    pl.when(has_down)(up.wait_recv)
    pl.when(has_up)(down.wait_recv)
    base = (b * N_LEAF + l) * LEAVES - LEAVES

    def near_rest(g, _):
        lhs = jnp.concatenate([x[jnp.clip(nlist[g, k] - base, 0, 3 * LEAVES - 1)] for k in range(1, NEAR)], axis=1)
        prod[g] = prod[g] + mm(lhs, near_w[g, pl.ds(SIZE, (NEAR - 1) * SIZE), :])
        return 0

    lax.fori_loop(0, LEAVES, near_rest, 0)

    for name in ("y_p", "zp_p", "zm_p"):
        copies[name].wait_recv()
    couple([(1, 0, 1), (0, -1, 1), (0, 1, 1), (1, -1, 0), (1, 1, 0), (0, 2, 0)], False)

    copies["yzp_fwd"].wait_recv()
    copies["yzm_fwd"].wait_recv()
    send("yz2_p", bufs[1, 2, 0], (1, 2, 1), whole, 0, 0, 1)

    g = split(mm3(lt_h[...], lt_l[...], t_h[...], t_l[...]))
    g_h[...], g_l[...] = g

    for name in ("yzp_p", "yzm_p", "z2_p"):
        copies[name].wait_recv()
    couple([(1, -1, 1), (1, 1, 1), (0, 2, 1), (1, 2, 0)], False)
    copies["yz2_p"].wait_recv()
    couple([(1, 2, 1)], False)

    for c in al:
        c.wait_recv()
    r_h, r_l = split(rf[...].reshape(NRHS, RANK))
    down_leaf = mm3(r_h, r_l, g_h[...], g_l[...], mm_t)
    stores = []
    for g in range(LEAVES):
        leaf_total = (far_acc[g] + down_leaf[:, g * RANK:(g + 1) * RANK]).astype(bf16)
        prod[g] = prod[g] + mm_t(leaf_total, basis[g])
        c = pltpu.make_async_copy(prod.at[g], out.at[:, pl.ds(g * SIZE, SIZE)], osem.at[g])
        c.start()
        stores.append(c)

    for c in list(copies.values()) + rs + ag + al:
        c.wait_send()
    pl.when(has_up)(up.wait_send)
    pl.when(has_down)(down.wait_send)
    for c in stores:
        c.wait()


def on_device(rhs, basis, near_list, near_block, local_transfer, cross_transfer, coupling_list, leaf_coupling, root_coupling):
    near_w = near_block.reshape(LEAVES, NEAR * SIZE, SIZE)
    coup = leaf_coupling.reshape(LEAVES, STEPS, SLOTS * RANK, RANK)
    rc = root_coupling.reshape(STEPS * RANK, RANK)
    V, S = pltpu.VMEM, pltpu.SemaphoreType
    dma = S.DMA
    scratch = [
        V((3 * LEAVES, NRHS, SIZE), bf16),
        V((LEAVES, SIZE, RANK), bf16),
        pltpu.SMEM((LEAVES, NEAR), jnp.int32),
        V((LEAVES, NEAR * SIZE, SIZE), bf16),
        V((LEAVES, RANK, RANK), f32),
        V((3, RANK, RANK), f32),
        pltpu.SMEM((LEAVES, SLOTS, STEPS), jnp.int32),
        V((LEAVES, STEPS, SLOTS * RANK, RANK), bf16),
        V((STEPS * RANK, RANK), bf16),
        V((LEAVES, NRHS, RANK), bf16),
        V((N_LEAF, ROWS, RANK), f32),
        V((N_LEAF - 1, ROWS, RANK), f32),
        V((ROWS, RANK), f32),
        V((STEPS, ROWS, RANK), f32),
        V((N_LEAF, ROWS, RANK), f32),
        V((LEAVES, NRHS, RANK), f32),
        V((LEAVES, NRHS, SIZE), f32),
        V((LEAVES * RANK, RANK), bf16),
        V((LEAVES * RANK, RANK), bf16),
        V((RANK, RANK), bf16),
        V((RANK, RANK), bf16),
        V((LEAVES * RANK, RANK), bf16),
        V((LEAVES * RANK, RANK), bf16),
    ]
    scratch += [V((LEAVES + 1, NRHS, RANK), bf16) for _ in SOURCES]
    scratch += [
        dma((32,)), dma((LEAVES,)), S.REGULAR, dma((2,)), dma((2,)), dma((17,)), dma((17,)),
        dma((7,)), dma((7,)), dma((15,)), dma((15,)), dma((7,)), dma((7,)),
    ]
    hbm = pl.BlockSpec(memory_space=pltpu.MemorySpace.HBM)
    return pl.pallas_call(
        kernel,
        out_shape=jax.ShapeDtypeStruct((NRHS, LEAVES * SIZE), f32),
        in_specs=[hbm] * 9,
        out_specs=pl.BlockSpec(memory_space=pltpu.VMEM),
        scratch_shapes=scratch,
        compiler_params=pltpu.CompilerParams(
            collective_id=0, has_side_effects=True, vmem_limit_bytes=67043328
        ),
    )(rhs, basis, near_list, near_w, local_transfer, cross_transfer, coupling_list.transpose(0, 2, 1), coup, rc)


def solution(mesh):
    both = ("blk", "leaf")
    in_specs = (
        P(None, both), P(both, None, None), P(both, None), P(both, None, None, None), P(both, None, None),
        P("blk", None, None, None), P(both, None, None), P(both, None, None, None, None), P("blk", None, None, None),
    )
    return jax.shard_map(on_device, mesh=mesh, in_specs=in_specs, out_specs=P(None, both), check_vma=False)
```

```python
import jax
import jax.numpy as jnp
from jax import lax
from jax.experimental import pallas as pl
from jax.experimental.pallas import tpu as pltpu
from jax.sharding import PartitionSpec as P

bf16, f32 = jnp.bfloat16, jnp.float32

N_BLK, N_LEAF = 16, 8
LEAVES, SIZE, RANK, NRHS = 8, 256, 128, 64
NEAR, SLOTS, STEPS = 6, 2, 15
ROWS = NRHS // N_LEAF

SOURCES = [
    (dy, dz, dc) for dz in (0, -1, 1, 2) for dy in (0, 1) for dc in (0, 1) if (dy, dz, dc) != (0, 0, 0)
]


def mm(a, b):
    return jnp.dot(a, b, preferred_element_type=f32)


def mm_t(a, b):
    return lax.dot_general(a, b, (((1,), (1,)), ((), ())), preferred_element_type=f32)


def split(v):
    high = v.astype(bf16)
    return high, (v - high.astype(f32)).astype(bf16)


def mm3(a_high, a_low, b_high, b_low, product=mm):
    rows = a_high.shape[0]
    both = product(jnp.concatenate([a_high, a_low], axis=0), b_high)
    return both[:rows] + both[rows:] + product(a_high, b_low)


def kernel(
    rhs, basis_hbm, near_list, near_hbm, lt_hbm, ct_hbm, coupling_list, coup_hbm, rc_hbm,
    out,
    x, basis, nlist, near_w, lt, ct, clist, coup, rc,
    own, share_buf, rs_buf, root_own, vis, rf, far_acc, prod,
    lt_h, lt_l, t_h, t_l, g_h, g_l,
    *rest,
):
    bufs = dict(zip(SOURCES, rest[: len(SOURCES)]))
    lsem, osem, barrier_unused, hs, hr, cs, cr, rs_s, rs_r, ag_s, ag_r, al_s, al_r = rest[len(SOURCES):]
    b = lax.axis_index("blk")
    l = lax.axis_index("leaf")
    core = b % 2
    z = (b // 2) % 4
    y = b // 8

    def blk_of(dy, dz, dc):
        yy = (y + dy) % 2
        zz = (z + dz + 4) % 4
        cc = (core + dc) % 2
        return yy * 8 + zz * 2 + cc

    barrier = pltpu.get_barrier_semaphore()
    for s in range(1, N_BLK):
        pl.semaphore_signal(barrier, inc=1, device_id={"blk": (b + s) % N_BLK})
    for d in range(1, N_LEAF):
        pl.semaphore_signal(barrier, inc=1, device_id={"leaf": (l + d) % N_LEAF})

    def load(src, dst, i):
        c = pltpu.make_async_copy(src, dst, lsem.at[i])
        c.start()
        return c

    x_loads = [
        load(rhs.at[:, pl.ds(g * SIZE, SIZE)], x.at[LEAVES + g], g) for g in range(LEAVES)
    ]
    basis_load = load(basis_hbm, basis, 8)
    ct_loads = [
        load(ct_hbm.at[0, 6 + l], ct.at[0], 9),
        load(ct_hbm.at[0, 2 + l // 2], ct.at[1], 10),
        load(ct_hbm.at[0, l // 4], ct.at[2], 11),
    ]
    lt_load = load(lt_hbm, lt, 12)
    nlist_load = load(near_list, nlist, 13)
    clist_load = load(coupling_list, clist, 14)

    for src in SOURCES:
        bufs[src][LEAVES] = jnp.zeros((NRHS, RANK), bf16)

    for c in x_loads:
        c.wait()
    basis_load.wait()
    for c in ct_loads:
        c.wait()
    lt_load.wait()
    near_loads = [load(near_hbm.at[g], near_w.at[g], 15 + g) for g in range(LEAVES)]
    rc_load = load(rc_hbm, rc, 23)
    coup_loads = [load(coup_hbm.at[g], coup.at[g], 24 + g) for g in range(LEAVES)]
    coef = []
    for g in range(LEAVES):
        c = mm(x[LEAVES + g], basis[g])
        coef.append(c)
        own[g] = c.astype(bf16)
    m0, m1, m2 = [split(ct[i]) for i in range(3)]
    t = split(mm3(*m0, *m1))
    t = split(mm3(*t, *m2))
    t_h[...], t_l[...] = t

    def blk_copy(src, dst, i, dy, dz, dc):
        return pltpu.make_async_remote_copy(
            src_ref=src, dst_ref=dst, send_sem=cs.at[i], recv_sem=cr.at[i],
            device_id={"blk": blk_of(dy, dz, dc)},
        )

    whole = pl.ds(0, LEAVES)
    first, second = pl.ds(0, LEAVES // 2), pl.ds(LEAVES // 2, LEAVES // 2)
    copies = {}

    def send(name, src, target, part, dy, dz, dc):
        i = len(copies)
        c = blk_copy(src.at[part], bufs[target].at[part], i, dy, dz, dc)
        copies[name] = c
        c.start()

    pl.semaphore_wait(barrier, N_BLK - 1 + N_LEAF - 1)
    send("zp", own, (0, -1, 0), whole, 0, 1, 0)
    send("zm", own, (0, 1, 0), whole, 0, -1, 0)
    send("p", own, (0, 0, 1), whole, 0, 0, 1)

    w_h, w_l = split(lt[...].reshape(LEAVES * RANK, RANK))
    lt_h[...] = w_h
    lt_l[...] = w_l
    parts = [split(c) for c in coef]
    c_h = jnp.concatenate([p[0] for p in parts], axis=1)
    c_l = jnp.concatenate([p[1] for p in parts], axis=1)
    node = mm3(c_h, c_l, lt_h[...], lt_l[...])
    share = mm3(*split(node), *t)
    share_buf[...] = share.reshape(N_LEAF, ROWS, RANK)

    rs = []
    for d in range(1, N_LEAF):
        to = (l + d) % N_LEAF
        c = pltpu.make_async_remote_copy(
            src_ref=share_buf.at[to], dst_ref=rs_buf.at[d - 1],
            send_sem=rs_s.at[d - 1], recv_sem=rs_r.at[d - 1], device_id={"leaf": to},
        )
        c.start()
        rs.append(c)
    send("y", own, (1, 0, 0), whole, 1, 0, 0)

    mine, low, high = pl.ds(LEAVES, LEAVES), pl.ds(0, LEAVES), pl.ds(2 * LEAVES, LEAVES)
    up = pltpu.make_async_remote_copy(
        src_ref=x.at[mine], dst_ref=x.at[low], send_sem=hs.at[0], recv_sem=hr.at[0],
        device_id={"leaf": (l + 1) % N_LEAF},
    )
    down = pltpu.make_async_remote_copy(
        src_ref=x.at[mine], dst_ref=x.at[high], send_sem=hs.at[1], recv_sem=hr.at[1],
        device_id={"leaf": (l + N_LEAF - 1) % N_LEAF},
    )
    has_up, has_down = l < N_LEAF - 1, l > 0
    pl.when(has_up)(up.start)
    pl.when(has_down)(down.start)

    for c in near_loads:
        c.wait()

    def near_own(g, _):
        prod[g] = mm(x[LEAVES + g], near_w[g, pl.ds(0, SIZE), :])
        return 0

    lax.fori_loop(0, LEAVES, near_own, 0, unroll=True)

    copies["zp"].wait_recv()
    send("zp_fwd", bufs[0, -1, 0], (0, 2, 0), first, 0, 1, 0)
    send("zp_p", bufs[0, -1, 0], (0, -1, 1), whole, 0, 0, 1)
    copies["zm"].wait_recv()
    send("zm_fwd", bufs[0, 1, 0], (0, 2, 0), second, 0, -1, 0)
    send("zm_p", bufs[0, 1, 0], (0, 1, 1), whole, 0, 0, 1)

    total = share_buf[l]
    for d in range(1, N_LEAF):
        rs[d - 1].wait_recv()
        total = total + rs_buf[d - 1]
    root_own[...] = total.astype(bf16).astype(f32)
    ag = []
    for s in range(1, N_BLK):
        c = pltpu.make_async_remote_copy(
            src_ref=root_own, dst_ref=vis.at[s - 1],
            send_sem=ag_s.at[s - 1], recv_sem=ag_r.at[s - 1], device_id={"blk": (b + s) % N_BLK},
        )
        c.start()
        ag.append(c)

    copies["y"].wait_recv()
    send("yzp", bufs[1, 0, 0], (1, -1, 0), whole, 0, 1, 0)
    send("yzm", bufs[1, 0, 0], (1, 1, 0), whole, 0, -1, 0)
    send("y_p", bufs[1, 0, 0], (1, 0, 1), whole, 0, 0, 1)

    clist_load.wait()
    for c in coup_loads:
        c.wait()

    def couple(sources, fresh):
        offsets = [(b - blk_of(*src) + N_BLK) % N_BLK - 1 for src in sources]

        def body(g, _):
            total = None if fresh else far_acc[g]
            for src, o in zip(sources, offsets):
                buf = bufs[src]
                lhs = jnp.concatenate([buf[clist[g, 0, o]], buf[clist[g, 1, o]]], axis=1)
                term = mm(lhs, coup[g, o])
                total = term if total is None else total + term
            far_acc[g] = total
            return 0

        lax.fori_loop(0, LEAVES, body, 0, unroll=2)

    copies["p"].wait_recv()
    couple([(0, 0, 1), (1, 0, 0), (0, -1, 0), (0, 1, 0)], True)

    copies["zp_fwd"].wait_recv()
    copies["zm_fwd"].wait_recv()
    send("z2_y", bufs[0, 2, 0], (1, 2, 0), whole, 1, 0, 0)
    send("z2_p", bufs[0, 2, 0], (0, 2, 1), whole, 0, 0, 1)

    for name in ("y_p", "zp_p", "zm_p"):
        copies[name].wait_recv()
    couple([(1, 0, 1), (0, -1, 1), (0, 1, 1)], False)

    rc_load.wait()
    for c in ag:
        c.wait_recv()
    lhs = jnp.concatenate([vis[s].astype(bf16) for s in range(STEPS)], axis=1)
    rows = mm(lhs, rc[...])
    rf[l] = rows
    al = []
    for d in range(1, N_LEAF):
        c = pltpu.make_async_remote_copy(
            src_ref=rf.at[l], dst_ref=rf.at[l],
            send_sem=al_s.at[d - 1], recv_sem=al_r.at[d - 1], device_id={"leaf": (l + d) % N_LEAF},
        )
        c.start()
        al.append(c)

    g = split(mm3(lt_h[...], lt_l[...], t_h[...], t_l[...]))
    g_h[...], g_l[...] = g

    copies["yzp"].wait_recv()
    send("yzp_p", bufs[1, -1, 0], (1, -1, 1), whole, 0, 0, 1)
    copies["yzm"].wait_recv()
    send("yzm_p", bufs[1, 1, 0], (1, 1, 1), whole, 0, 0, 1)

    nlist_load.wait()
    pl.when(has_down)(up.wait_recv)
    pl.when(has_up)(down.wait_recv)
    base = (b * N_LEAF + l) * LEAVES - LEAVES

    def near_rest(g, _):
        lhs = jnp.concatenate([x[jnp.clip(nlist[g, k] - base, 0, 3 * LEAVES - 1)] for k in range(1, NEAR)], axis=1)
        prod[g] = prod[g] + mm(lhs, near_w[g, pl.ds(SIZE, (NEAR - 1) * SIZE), :])
        return 0

    lax.fori_loop(0, LEAVES, near_rest, 0, unroll=2)

    copies["z2_y"].wait_recv()
    send("yz2_p", bufs[1, 2, 0], (1, 2, 1), whole, 0, 0, 1)

    for name in ("z2_p", "yzp_p", "yzm_p"):
        copies[name].wait_recv()
    couple(
        [(1, -1, 0), (1, 1, 0), (0, 2, 0), (0, 2, 1), (1, -1, 1), (1, 1, 1), (1, 2, 0)], False
    )

    for c in al:
        c.wait_recv()
    r_h, r_l = split(rf[...].reshape(NRHS, RANK))
    down_leaf = mm3(r_h, r_l, g_h[...], g_l[...], mm_t)
    for g in range(LEAVES):
        far_acc[g] = far_acc[g] + down_leaf[:, g * RANK:(g + 1) * RANK]
    copies["yz2_p"].wait_recv()
    last = bufs[1, 2, 1]
    o = (b - blk_of(1, 2, 1) + N_BLK) % N_BLK - 1
    stores = []
    for g in range(LEAVES):
        lhs = jnp.concatenate([last[clist[g, 0, o]], last[clist[g, 1, o]]], axis=1)
        leaf_total = (far_acc[g] + mm(lhs, coup[g, o])).astype(bf16)
        prod[g] = prod[g] + mm_t(leaf_total, basis[g])
        c = pltpu.make_async_copy(prod.at[g], out.at[:, pl.ds(g * SIZE, SIZE)], osem.at[g])
        c.start()
        stores.append(c)

    for c in list(copies.values()) + rs + ag + al:
        c.wait_send()
    pl.when(has_up)(up.wait_send)
    pl.when(has_down)(down.wait_send)
    for c in stores:
        c.wait()


def on_device(rhs, basis, near_list, near_block, local_transfer, cross_transfer, coupling_list, leaf_coupling, root_coupling):
    near_w = near_block.reshape(LEAVES, NEAR * SIZE, SIZE)
    coup = leaf_coupling.reshape(LEAVES, STEPS, SLOTS * RANK, RANK)
    rc = root_coupling.reshape(STEPS * RANK, RANK)
    V, S = pltpu.VMEM, pltpu.SemaphoreType
    dma = S.DMA
    scratch = [
        V((3 * LEAVES, NRHS, SIZE), bf16),
        V((LEAVES, SIZE, RANK), bf16),
        pltpu.SMEM((LEAVES, NEAR), jnp.int32),
        V((LEAVES, NEAR * SIZE, SIZE), bf16),
        V((LEAVES, RANK, RANK), f32),
        V((3, RANK, RANK), f32),
        pltpu.SMEM((LEAVES, SLOTS, STEPS), jnp.int32),
        V((LEAVES, STEPS, SLOTS * RANK, RANK), bf16),
        V((STEPS * RANK, RANK), bf16),
        V((LEAVES, NRHS, RANK), bf16),
        V((N_LEAF, ROWS, RANK), f32),
        V((N_LEAF - 1, ROWS, RANK), f32),
        V((ROWS, RANK), f32),
        V((STEPS, ROWS, RANK), f32),
        V((N_LEAF, ROWS, RANK), f32),
        V((LEAVES, NRHS, RANK), f32),
        V((LEAVES, NRHS, SIZE), f32),
        V((LEAVES * RANK, RANK), bf16),
        V((LEAVES * RANK, RANK), bf16),
        V((RANK, RANK), bf16),
        V((RANK, RANK), bf16),
        V((LEAVES * RANK, RANK), bf16),
        V((LEAVES * RANK, RANK), bf16),
    ]
    scratch += [V((LEAVES + 1, NRHS, RANK), bf16) for _ in SOURCES]
    scratch += [
        dma((32,)), dma((LEAVES,)), S.REGULAR, dma((2,)), dma((2,)), dma((17,)), dma((17,)),
        dma((7,)), dma((7,)), dma((15,)), dma((15,)), dma((7,)), dma((7,)),
    ]
    hbm = pl.BlockSpec(memory_space=pltpu.MemorySpace.HBM)
    return pl.pallas_call(
        kernel,
        out_shape=jax.ShapeDtypeStruct((NRHS, LEAVES * SIZE), f32),
        in_specs=[hbm] * 9,
        out_specs=hbm,
        scratch_shapes=scratch,
        compiler_params=pltpu.CompilerParams(
            collective_id=0, has_side_effects=True, vmem_limit_bytes=67043328
        ),
    )(rhs, basis, near_list, near_w, local_transfer, cross_transfer, coupling_list.transpose(0, 2, 1), coup, rc)


def solution(mesh):
    both = ("blk", "leaf")
    in_specs = (
        P(None, both), P(both, None, None), P(both, None), P(both, None, None, None), P(both, None, None),
        P("blk", None, None, None), P(both, None, None), P(both, None, None, None, None), P("blk", None, None, None),
    )
    return jax.shard_map(on_device, mesh=mesh, in_specs=in_specs, out_specs=P(None, both), check_vma=False)
```

```python
import jax
import jax.numpy as jnp
from jax import lax
from jax.experimental import pallas as pl
from jax.experimental.pallas import tpu as pltpu
from jax.sharding import PartitionSpec as P

bf16, f32 = jnp.bfloat16, jnp.float32

N_BLK, N_LEAF = 16, 8
LEAVES, SIZE, RANK, NRHS = 8, 256, 128, 64
NEAR, SLOTS, STEPS = 6, 2, 15
ROWS = NRHS // N_LEAF

SOURCES = [
    (dy, dz, dc) for dz in (0, -1, 1, 2) for dy in (0, 1) for dc in (0, 1) if (dy, dz, dc) != (0, 0, 0)
]


def mm(a, b):
    return jnp.dot(a, b, preferred_element_type=f32)


def mm_t(a, b):
    return lax.dot_general(a, b, (((1,), (1,)), ((), ())), preferred_element_type=f32)


def split(v):
    high = v.astype(bf16)
    return high, (v - high.astype(f32)).astype(bf16)


def mm3(a_high, a_low, b_high, b_low, product=mm):
    rows = a_high.shape[0]
    both = product(jnp.concatenate([a_high, a_low], axis=0), b_high)
    return both[:rows] + both[rows:] + product(a_high, b_low)


def kernel(
    rhs, basis_hbm, near_list, near_hbm, lt_hbm, ct_hbm, coupling_list, coup_hbm, rc_hbm,
    out,
    x, basis, nlist, near_w, lt, ct, clist, coup, rc,
    own, share_buf, rs_buf, root_own, vis, rf, far_acc, prod,
    lt_h, lt_l, t_h, t_l, g_h, g_l, relay_buf, xs, xr,
    *rest,
):
    bufs = dict(zip(SOURCES, rest[: len(SOURCES)]))
    lsem, osem, barrier_unused, hs, hr, cs, cr, rs_s, rs_r, ag_s, ag_r, al_s, al_r = rest[len(SOURCES):]
    b = lax.axis_index("blk")
    l = lax.axis_index("leaf")
    core = b % 2
    z = (b // 2) % 4
    y = b // 8

    def blk_of(dy, dz, dc):
        yy = (y + dy) % 2
        zz = (z + dz + 4) % 4
        cc = (core + dc) % 2
        return yy * 8 + zz * 2 + cc

    barrier = pltpu.get_barrier_semaphore()
    for s in range(1, N_BLK):
        pl.semaphore_signal(barrier, inc=1, device_id={"blk": (b + s) % N_BLK})
    for d in range(1, N_LEAF):
        pl.semaphore_signal(barrier, inc=1, device_id={"leaf": (l + d) % N_LEAF})
        pl.semaphore_signal(barrier, inc=1, device_id={"blk": blk_of(1, 0, 0), "leaf": (l + d) % N_LEAF})

    def load(src, dst, i):
        c = pltpu.make_async_copy(src, dst, lsem.at[i])
        c.start()
        return c

    x_loads = [
        load(rhs.at[:, pl.ds(g * SIZE, SIZE)], x.at[LEAVES + g], g) for g in range(LEAVES)
    ]
    basis_load = load(basis_hbm, basis, 8)
    ct_loads = [
        load(ct_hbm.at[0, 6 + l], ct.at[0], 9),
        load(ct_hbm.at[0, 2 + l // 2], ct.at[1], 10),
        load(ct_hbm.at[0, l // 4], ct.at[2], 11),
    ]
    lt_load = load(lt_hbm, lt, 12)
    nlist_load = load(near_list, nlist, 13)
    clist_load = load(coupling_list, clist, 14)

    for src in SOURCES:
        bufs[src][LEAVES] = jnp.zeros((NRHS, RANK), bf16)

    for c in x_loads:
        c.wait()
    basis_load.wait()
    for c in ct_loads:
        c.wait()
    lt_load.wait()
    near_loads = [load(near_hbm.at[g], near_w.at[g], 15 + g) for g in range(LEAVES)]
    rc_load = load(rc_hbm, rc, 23)
    coup_loads = [load(coup_hbm.at[g], coup.at[g], 24 + g) for g in range(LEAVES)]
    coef = []
    for g in range(LEAVES):
        c = mm(x[LEAVES + g], basis[g])
        coef.append(c)
        own[g] = c.astype(bf16)
    m0, m1, m2 = [split(ct[i]) for i in range(3)]
    t = split(mm3(*m0, *m1))
    t = split(mm3(*t, *m2))
    t_h[...], t_l[...] = t

    def blk_copy(src, dst, i, dy, dz, dc):
        return pltpu.make_async_remote_copy(
            src_ref=src, dst_ref=dst, send_sem=cs.at[i], recv_sem=cr.at[i],
            device_id={"blk": blk_of(dy, dz, dc)},
        )

    whole = pl.ds(0, LEAVES)
    first, second = pl.ds(0, LEAVES // 2), pl.ds(LEAVES // 2, LEAVES // 2)
    copies = {}

    def send(name, src, target, part, dy, dz, dc):
        i = len(copies)
        c = blk_copy(src.at[part], bufs[target].at[part], i, dy, dz, dc)
        copies[name] = c
        c.start()

    pl.semaphore_wait(barrier, N_BLK - 1 + 2 * (N_LEAF - 1))
    send("zp", own, (0, -1, 0), whole, 0, 1, 0)
    send("zm", own, (0, 1, 0), whole, 0, -1, 0)
    send("p", own, (0, 0, 1), whole, 0, 0, 1)

    w_h, w_l = split(lt[...].reshape(LEAVES * RANK, RANK))
    lt_h[...] = w_h
    lt_l[...] = w_l
    parts = [split(c) for c in coef]
    c_h = jnp.concatenate([p[0] for p in parts], axis=1)
    c_l = jnp.concatenate([p[1] for p in parts], axis=1)
    node = mm3(c_h, c_l, lt_h[...], lt_l[...])
    share = mm3(*split(node), *t)
    share_buf[...] = share.reshape(N_LEAF, ROWS, RANK)

    rs = []
    for d in range(1, N_LEAF):
        to = (l + d) % N_LEAF
        c = pltpu.make_async_remote_copy(
            src_ref=share_buf.at[to], dst_ref=rs_buf.at[d - 1],
            send_sem=rs_s.at[d - 1], recv_sem=rs_r.at[d - 1], device_id={"leaf": to},
        )
        c.start()
        rs.append(c)
    send("y", own, (1, 0, 0), whole, 1, 0, 0)

    mine, low, high = pl.ds(LEAVES, LEAVES), pl.ds(0, LEAVES), pl.ds(2 * LEAVES, LEAVES)
    up = pltpu.make_async_remote_copy(
        src_ref=x.at[mine], dst_ref=x.at[low], send_sem=hs.at[0], recv_sem=hr.at[0],
        device_id={"leaf": (l + 1) % N_LEAF},
    )
    down = pltpu.make_async_remote_copy(
        src_ref=x.at[mine], dst_ref=x.at[high], send_sem=hs.at[1], recv_sem=hr.at[1],
        device_id={"leaf": (l + N_LEAF - 1) % N_LEAF},
    )
    mid = N_LEAF // 2
    has_up, has_down = (l < N_LEAF - 1) & (l != mid - 1), (l > 0) & (l != mid)
    crosses = (l == mid - 1) | (l == mid)
    goes_up = l == mid - 1
    relays = (l % mid == 0) | (l % mid == mid - 1)
    relay_up = l % mid == 0
    y_blk = blk_of(1, 0, 0)
    relay_leaf = [
        jnp.where(goes_up, jnp.where(y == h, mid, 0), jnp.where(y == h, mid - 1, N_LEAF - 1)) for h in range(2)
    ]
    crossing = [
        pltpu.make_async_remote_copy(
            src_ref=x.at[pl.ds(LEAVES + h * (LEAVES // 2), LEAVES // 2)], dst_ref=relay_buf,
            send_sem=xs.at[h], recv_sem=xr.at[0], device_id={"blk": y_blk, "leaf": relay_leaf[h]},
        )
        for h in range(2)
    ]
    half = jnp.where(relay_up, (y == 1) == (l == 0), (y == 1) != (l == mid - 1)).astype(jnp.int32)
    relay_to = jnp.where(relay_up, 0, 2 * LEAVES) + half * (LEAVES // 2)
    relayed = pltpu.make_async_remote_copy(
        src_ref=relay_buf, dst_ref=x.at[pl.ds(relay_to, LEAVES // 2)],
        send_sem=xs.at[2], recv_sem=xr.at[1 + half],
        device_id={"blk": y_blk, "leaf": jnp.where(relay_up, mid, mid - 1)},
    )
    arrivals = [
        pltpu.make_async_remote_copy(
            src_ref=relay_buf, dst_ref=x.at[pl.ds(jnp.where(goes_up, 2 * LEAVES, 0) + h * (LEAVES // 2), LEAVES // 2)],
            send_sem=xs.at[2], recv_sem=xr.at[1 + h], device_id={"blk": y_blk, "leaf": l},
        )
        for h in range(2)
    ]
    pl.when(has_up)(up.start)
    pl.when(has_down)(down.start)

    @pl.when(crosses)
    def _():
        for c in crossing:
            c.start()

    for c in near_loads:
        c.wait()

    def near_own(g, _):
        prod[g] = mm(x[LEAVES + g], near_w[g, pl.ds(0, SIZE), :])
        return 0

    lax.fori_loop(0, LEAVES, near_own, 0, unroll=True)

    copies["zp"].wait_recv()
    send("zp_fwd", bufs[0, -1, 0], (0, 2, 0), first, 0, 1, 0)
    send("zp_p", bufs[0, -1, 0], (0, -1, 1), whole, 0, 0, 1)
    copies["zm"].wait_recv()
    send("zm_fwd", bufs[0, 1, 0], (0, 2, 0), second, 0, -1, 0)
    send("zm_p", bufs[0, 1, 0], (0, 1, 1), whole, 0, 0, 1)

    total = share_buf[l]
    for d in range(1, N_LEAF):
        rs[d - 1].wait_recv()
        total = total + rs_buf[d - 1]
    root_own[...] = total.astype(bf16).astype(f32)
    ag = []
    for s in range(1, N_BLK):
        c = pltpu.make_async_remote_copy(
            src_ref=root_own, dst_ref=vis.at[s - 1],
            send_sem=ag_s.at[s - 1], recv_sem=ag_r.at[s - 1], device_id={"blk": (b + s) % N_BLK},
        )
        c.start()
        ag.append(c)

    copies["y"].wait_recv()
    send("yzp", bufs[1, 0, 0], (1, -1, 0), whole, 0, 1, 0)
    send("yzm", bufs[1, 0, 0], (1, 1, 0), whole, 0, -1, 0)
    send("y_p", bufs[1, 0, 0], (1, 0, 1), whole, 0, 0, 1)

    clist_load.wait()
    for c in coup_loads:
        c.wait()

    def couple(sources, fresh):
        offsets = [(b - blk_of(*src) + N_BLK) % N_BLK - 1 for src in sources]

        def body(g, _):
            total = None if fresh else far_acc[g]
            for src, o in zip(sources, offsets):
                buf = bufs[src]
                lhs = jnp.concatenate([buf[clist[g, 0, o]], buf[clist[g, 1, o]]], axis=1)
                term = mm(lhs, coup[g, o])
                total = term if total is None else total + term
            far_acc[g] = total
            return 0

        lax.fori_loop(0, LEAVES, body, 0, unroll=2)

    copies["p"].wait_recv()
    couple([(0, 0, 1), (1, 0, 0), (0, -1, 0), (0, 1, 0)], True)

    copies["zp_fwd"].wait_recv()
    copies["zm_fwd"].wait_recv()
    send("z2_y", bufs[0, 2, 0], (1, 2, 0), whole, 1, 0, 0)
    send("z2_p", bufs[0, 2, 0], (0, 2, 1), whole, 0, 0, 1)

    for name in ("y_p", "zp_p", "zm_p"):
        copies[name].wait_recv()
    couple([(1, 0, 1), (0, -1, 1), (0, 1, 1)], False)

    rc_load.wait()
    for c in ag:
        c.wait_recv()
    lhs = jnp.concatenate([vis[s].astype(bf16) for s in range(STEPS)], axis=1)
    rows = mm(lhs, rc[...])
    rf[l] = rows
    al = []
    for d in range(1, N_LEAF):
        c = pltpu.make_async_remote_copy(
            src_ref=rf.at[l], dst_ref=rf.at[l],
            send_sem=al_s.at[d - 1], recv_sem=al_r.at[d - 1], device_id={"leaf": (l + d) % N_LEAF},
        )
        c.start()
        al.append(c)

    @pl.when(relays)
    def _():
        crossing[0].wait_recv()
        relayed.start()

    g = split(mm3(lt_h[...], lt_l[...], t_h[...], t_l[...]))
    g_h[...], g_l[...] = g

    copies["yzp"].wait_recv()
    send("yzp_p", bufs[1, -1, 0], (1, -1, 1), whole, 0, 0, 1)
    copies["yzm"].wait_recv()
    send("yzm_p", bufs[1, 1, 0], (1, 1, 1), whole, 0, 0, 1)

    nlist_load.wait()
    pl.when(has_down)(up.wait_recv)
    pl.when(has_up)(down.wait_recv)

    @pl.when(crosses)
    def _():
        for c in arrivals:
            c.wait_recv()

    base = (b * N_LEAF + l) * LEAVES - LEAVES

    def near_rest(g, _):
        lhs = jnp.concatenate([x[jnp.clip(nlist[g, k] - base, 0, 3 * LEAVES - 1)] for k in range(1, NEAR)], axis=1)
        prod[g] = prod[g] + mm(lhs, near_w[g, pl.ds(SIZE, (NEAR - 1) * SIZE), :])
        return 0

    lax.fori_loop(0, LEAVES, near_rest, 0, unroll=2)

    copies["z2_y"].wait_recv()
    send("yz2_p", bufs[1, 2, 0], (1, 2, 1), whole, 0, 0, 1)

    for name in ("z2_p", "yzp_p", "yzm_p"):
        copies[name].wait_recv()
    couple(
        [(1, -1, 0), (1, 1, 0), (0, 2, 0), (0, 2, 1), (1, -1, 1), (1, 1, 1), (1, 2, 0)], False
    )

    for c in al:
        c.wait_recv()
    r_h, r_l = split(rf[...].reshape(NRHS, RANK))
    down_leaf = mm3(r_h, r_l, g_h[...], g_l[...], mm_t)
    for g in range(LEAVES):
        far_acc[g] = far_acc[g] + down_leaf[:, g * RANK:(g + 1) * RANK]
    copies["yz2_p"].wait_recv()
    last = bufs[1, 2, 1]
    o = (b - blk_of(1, 2, 1) + N_BLK) % N_BLK - 1
    stores = []
    for g in range(LEAVES):
        lhs = jnp.concatenate([last[clist[g, 0, o]], last[clist[g, 1, o]]], axis=1)
        leaf_total = (far_acc[g] + mm(lhs, coup[g, o])).astype(bf16)
        prod[g] = prod[g] + mm_t(leaf_total, basis[g])
        c = pltpu.make_async_copy(prod.at[g], out.at[:, pl.ds(g * SIZE, SIZE)], osem.at[g])
        c.start()
        stores.append(c)

    for c in list(copies.values()) + rs + ag + al:
        c.wait_send()
    pl.when(has_up)(up.wait_send)
    pl.when(has_down)(down.wait_send)

    @pl.when(crosses)
    def _():
        for c in crossing:
            c.wait_send()

    pl.when(relays)(relayed.wait_send)
    for c in stores:
        c.wait()


def on_device(rhs, basis, near_list, near_block, local_transfer, cross_transfer, coupling_list, leaf_coupling, root_coupling):
    near_w = near_block.reshape(LEAVES, NEAR * SIZE, SIZE)
    coup = leaf_coupling.reshape(LEAVES, STEPS, SLOTS * RANK, RANK)
    rc = root_coupling.reshape(STEPS * RANK, RANK)
    V, S = pltpu.VMEM, pltpu.SemaphoreType
    dma = S.DMA
    scratch = [
        V((3 * LEAVES, NRHS, SIZE), bf16),
        V((LEAVES, SIZE, RANK), bf16),
        pltpu.SMEM((LEAVES, NEAR), jnp.int32),
        V((LEAVES, NEAR * SIZE, SIZE), bf16),
        V((LEAVES, RANK, RANK), f32),
        V((3, RANK, RANK), f32),
        pltpu.SMEM((LEAVES, SLOTS, STEPS), jnp.int32),
        V((LEAVES, STEPS, SLOTS * RANK, RANK), bf16),
        V((STEPS * RANK, RANK), bf16),
        V((LEAVES, NRHS, RANK), bf16),
        V((N_LEAF, ROWS, RANK), f32),
        V((N_LEAF - 1, ROWS, RANK), f32),
        V((ROWS, RANK), f32),
        V((STEPS, ROWS, RANK), f32),
        V((N_LEAF, ROWS, RANK), f32),
        V((LEAVES, NRHS, RANK), f32),
        V((LEAVES, NRHS, SIZE), f32),
        V((LEAVES * RANK, RANK), bf16),
        V((LEAVES * RANK, RANK), bf16),
        V((RANK, RANK), bf16),
        V((RANK, RANK), bf16),
        V((LEAVES * RANK, RANK), bf16),
        V((LEAVES * RANK, RANK), bf16),
    ]
    scratch += [V((LEAVES // 2, NRHS, SIZE), bf16), dma((3,)), dma((3,))]
    scratch += [V((LEAVES + 1, NRHS, RANK), bf16) for _ in SOURCES]
    scratch += [
        dma((32,)), dma((LEAVES,)), S.REGULAR, dma((2,)), dma((2,)), dma((17,)), dma((17,)),
        dma((7,)), dma((7,)), dma((15,)), dma((15,)), dma((7,)), dma((7,)),
    ]
    hbm = pl.BlockSpec(memory_space=pltpu.MemorySpace.HBM)
    return pl.pallas_call(
        kernel,
        out_shape=jax.ShapeDtypeStruct((NRHS, LEAVES * SIZE), f32),
        in_specs=[hbm] * 9,
        out_specs=hbm,
        scratch_shapes=scratch,
        compiler_params=pltpu.CompilerParams(
            collective_id=0, has_side_effects=True, vmem_limit_bytes=67043328
        ),
    )(rhs, basis, near_list, near_w, local_transfer, cross_transfer, coupling_list.transpose(0, 2, 1), coup, rc)


def solution(mesh):
    both = ("blk", "leaf")
    in_specs = (
        P(None, both), P(both, None, None), P(both, None), P(both, None, None, None), P(both, None, None),
        P("blk", None, None, None), P(both, None, None), P(both, None, None, None, None), P("blk", None, None, None),
    )
    return jax.shard_map(on_device, mesh=mesh, in_specs=in_specs, out_specs=P(None, both), check_vma=False)
```

```python
import jax
import jax.numpy as jnp
from jax import lax
from jax.experimental import pallas as pl
from jax.experimental.pallas import tpu as pltpu
from jax.sharding import PartitionSpec as P

bf16, f32 = jnp.bfloat16, jnp.float32

N_BLK, N_LEAF = 16, 8
LEAVES, SIZE, RANK, NRHS = 8, 256, 128, 64
NEAR, SLOTS, STEPS = 6, 2, 15
ROWS = NRHS // N_LEAF

SOURCES = [
    (dy, dz, dc) for dz in (0, -1, 1, 2) for dy in (0, 1) for dc in (0, 1) if (dy, dz, dc) != (0, 0, 0)
]


def mm(a, b):
    return jnp.dot(a, b, preferred_element_type=f32)


def mm_t(a, b):
    return lax.dot_general(a, b, (((1,), (1,)), ((), ())), preferred_element_type=f32)


def split(v):
    high = v.astype(bf16)
    return high, (v - high.astype(f32)).astype(bf16)


def mm3(a_high, a_low, b_high, b_low, product=mm):
    rows = a_high.shape[0]
    both = product(jnp.concatenate([a_high, a_low], axis=0), b_high)
    return both[:rows] + both[rows:] + product(a_high, b_low)


def kernel(
    rhs, basis_hbm, near_list, near_hbm, lt_hbm, ct_hbm, coupling_list, coup_hbm, rc_hbm,
    out,
    x, basis, nlist, near_w, lt, ct, clist, coup, rc,
    own, share_buf, rs_buf, root_own, vis, rf, far_acc, prod,
    lt_h, lt_l, t_h, t_l, g_h, g_l, relay_buf, xs, xr,
    *rest,
):
    bufs = dict(zip(SOURCES, rest[: len(SOURCES)]))
    lsem, osem, barrier_unused, hs, hr, cs, cr, rs_s, rs_r, ag_s, ag_r, al_s, al_r = rest[len(SOURCES):]
    b = lax.axis_index("blk")
    l = lax.axis_index("leaf")
    core = b % 2
    z = (b // 2) % 4
    y = b // 8

    def blk_of(dy, dz, dc):
        yy = (y + dy) % 2
        zz = (z + dz + 4) % 4
        cc = (core + dc) % 2
        return yy * 8 + zz * 2 + cc

    barrier = pltpu.get_barrier_semaphore()
    for s in range(1, N_BLK):
        pl.semaphore_signal(barrier, inc=1, device_id={"blk": (b + s) % N_BLK})
    for d in range(1, N_LEAF):
        pl.semaphore_signal(barrier, inc=1, device_id={"leaf": (l + d) % N_LEAF})
        pl.semaphore_signal(barrier, inc=1, device_id={"blk": blk_of(1, 0, 0), "leaf": (l + d) % N_LEAF})

    def load(src, dst, i):
        c = pltpu.make_async_copy(src, dst, lsem.at[i])
        c.start()
        return c

    x_loads = [
        load(rhs.at[:, pl.ds(g * SIZE, SIZE)], x.at[LEAVES + g], g) for g in range(LEAVES)
    ]
    basis_load = load(basis_hbm, basis, 8)
    ct_loads = [
        load(ct_hbm.at[0, 6 + l], ct.at[0], 9),
        load(ct_hbm.at[0, 2 + l // 2], ct.at[1], 10),
        load(ct_hbm.at[0, l // 4], ct.at[2], 11),
    ]
    lt_load = load(lt_hbm, lt, 12)
    nlist_load = load(near_list, nlist, 13)
    clist_load = load(coupling_list, clist, 14)

    for src in SOURCES:
        bufs[src][LEAVES] = jnp.zeros((NRHS, RANK), bf16)

    for c in x_loads:
        c.wait()
    basis_load.wait()
    for c in ct_loads:
        c.wait()
    lt_load.wait()
    near_loads = [load(near_hbm.at[g], near_w.at[g], 15 + g) for g in range(LEAVES)]
    rc_load = load(rc_hbm, rc, 23)
    coup_loads = [load(coup_hbm.at[g], coup.at[g], 24 + g) for g in range(LEAVES)]
    coef = []
    for g in range(LEAVES):
        c = mm(x[LEAVES + g], basis[g])
        coef.append(c)
        own[g] = c.astype(bf16)
    m0, m1, m2 = [split(ct[i]) for i in range(3)]
    t = split(mm3(*m0, *m1))
    t = split(mm3(*t, *m2))
    t_h[...], t_l[...] = t

    def blk_copy(src, dst, i, dy, dz, dc):
        return pltpu.make_async_remote_copy(
            src_ref=src, dst_ref=dst, send_sem=cs.at[i], recv_sem=cr.at[i],
            device_id={"blk": blk_of(dy, dz, dc)},
        )

    whole = pl.ds(0, LEAVES)
    first, second = pl.ds(0, LEAVES // 2), pl.ds(LEAVES // 2, LEAVES // 2)
    copies = {}

    def send(name, src, target, part, dy, dz, dc):
        i = len(copies)
        c = blk_copy(src.at[part], bufs[target].at[part], i, dy, dz, dc)
        copies[name] = c
        c.start()

    pl.semaphore_wait(barrier, N_BLK - 1 + 2 * (N_LEAF - 1))
    send("zp", own, (0, -1, 0), whole, 0, 1, 0)
    send("zm", own, (0, 1, 0), whole, 0, -1, 0)
    send("p", own, (0, 0, 1), whole, 0, 0, 1)

    w_h, w_l = split(lt[...].reshape(LEAVES * RANK, RANK))
    lt_h[...] = w_h
    lt_l[...] = w_l
    parts = [split(c) for c in coef]
    c_h = jnp.concatenate([p[0] for p in parts], axis=1)
    c_l = jnp.concatenate([p[1] for p in parts], axis=1)
    node = mm3(c_h, c_l, lt_h[...], lt_l[...])
    share = mm3(*split(node), *t)
    share_buf[...] = share.reshape(N_LEAF, ROWS, RANK)

    rs = []
    for d in range(1, N_LEAF):
        to = (l + d) % N_LEAF
        c = pltpu.make_async_remote_copy(
            src_ref=share_buf.at[to], dst_ref=rs_buf.at[d - 1],
            send_sem=rs_s.at[d - 1], recv_sem=rs_r.at[d - 1], device_id={"leaf": to},
        )
        c.start()
        rs.append(c)
    send("y", own, (1, 0, 0), whole, 1, 0, 0)

    mine, low, high = pl.ds(LEAVES, LEAVES), pl.ds(0, LEAVES), pl.ds(2 * LEAVES, LEAVES)
    up = pltpu.make_async_remote_copy(
        src_ref=x.at[mine], dst_ref=x.at[low], send_sem=hs.at[0], recv_sem=hr.at[0],
        device_id={"leaf": (l + 1) % N_LEAF},
    )
    down = pltpu.make_async_remote_copy(
        src_ref=x.at[mine], dst_ref=x.at[high], send_sem=hs.at[1], recv_sem=hr.at[1],
        device_id={"leaf": (l + N_LEAF - 1) % N_LEAF},
    )
    mid = N_LEAF // 2
    has_up, has_down = (l < N_LEAF - 1) & (l != mid - 1), (l > 0) & (l != mid)
    crosses = (l == mid - 1) | (l == mid)
    goes_up = l == mid - 1
    relays = (l % mid == 0) | (l % mid == mid - 1)
    relay_up = l % mid == 0
    y_blk = blk_of(1, 0, 0)
    relay_leaf = [
        jnp.where(goes_up, jnp.where(y == h, mid, 0), jnp.where(y == h, mid - 1, N_LEAF - 1)) for h in range(2)
    ]
    crossing = [
        pltpu.make_async_remote_copy(
            src_ref=x.at[pl.ds(LEAVES + h * (LEAVES // 2) + 2 * q, 2)], dst_ref=relay_buf.at[pl.ds(2 * q, 2)],
            send_sem=xs.at[2 * q + h], recv_sem=xr.at[q], device_id={"blk": y_blk, "leaf": relay_leaf[h]},
        )
        for q in range(2) for h in range(2)
    ]
    half = jnp.where(relay_up, (y == 1) == (l == 0), (y == 1) != (l == mid - 1)).astype(jnp.int32)
    relay_to = jnp.where(relay_up, 0, 2 * LEAVES) + half * (LEAVES // 2)
    relayed = [
        pltpu.make_async_remote_copy(
            src_ref=relay_buf.at[pl.ds(2 * q, 2)], dst_ref=x.at[pl.ds(relay_to + 2 * q, 2)],
            send_sem=xs.at[4 + q], recv_sem=xr.at[2 + 2 * q + half],
            device_id={"blk": y_blk, "leaf": jnp.where(relay_up, mid, mid - 1)},
        )
        for q in range(2)
    ]

    def relay(q):
        @pl.when(relays)
        def _():
            crossing[2 * q].wait_recv()
            relayed[q].start()

    arrivals = [
        pltpu.make_async_remote_copy(
            src_ref=relay_buf.at[pl.ds(2 * q, 2)],
            dst_ref=x.at[pl.ds(jnp.where(goes_up, 2 * LEAVES, 0) + h * (LEAVES // 2) + 2 * q, 2)],
            send_sem=xs.at[4 + q], recv_sem=xr.at[2 + 2 * q + h], device_id={"blk": y_blk, "leaf": l},
        )
        for q in range(2) for h in range(2)
    ]
    pl.when(has_up)(up.start)
    pl.when(has_down)(down.start)

    @pl.when(crosses)
    def _():
        for c in crossing:
            c.start()

    for c in near_loads:
        c.wait()

    def near_own(g, _):
        prod[g] = mm(x[LEAVES + g], near_w[g, pl.ds(0, SIZE), :])
        return 0

    lax.fori_loop(0, LEAVES, near_own, 0, unroll=True)

    copies["zp"].wait_recv()
    send("zp_fwd", bufs[0, -1, 0], (0, 2, 0), first, 0, 1, 0)
    send("zp_p", bufs[0, -1, 0], (0, -1, 1), whole, 0, 0, 1)
    copies["zm"].wait_recv()
    send("zm_fwd", bufs[0, 1, 0], (0, 2, 0), second, 0, -1, 0)
    send("zm_p", bufs[0, 1, 0], (0, 1, 1), whole, 0, 0, 1)

    total = share_buf[l]
    for d in range(1, N_LEAF):
        rs[d - 1].wait_recv()
        total = total + rs_buf[d - 1]
    root_own[...] = total.astype(bf16).astype(f32)
    ag = []
    for s in range(1, N_BLK):
        c = pltpu.make_async_remote_copy(
            src_ref=root_own, dst_ref=vis.at[s - 1],
            send_sem=ag_s.at[s - 1], recv_sem=ag_r.at[s - 1], device_id={"blk": (b + s) % N_BLK},
        )
        c.start()
        ag.append(c)

    copies["y"].wait_recv()
    send("yzp", bufs[1, 0, 0], (1, -1, 0), whole, 0, 1, 0)
    send("yzm", bufs[1, 0, 0], (1, 1, 0), whole, 0, -1, 0)
    send("y_p", bufs[1, 0, 0], (1, 0, 1), whole, 0, 0, 1)

    clist_load.wait()
    for c in coup_loads:
        c.wait()

    def couple(sources, fresh):
        offsets = [(b - blk_of(*src) + N_BLK) % N_BLK - 1 for src in sources]

        def body(g, _):
            total = None if fresh else far_acc[g]
            for src, o in zip(sources, offsets):
                buf = bufs[src]
                lhs = jnp.concatenate([buf[clist[g, 0, o]], buf[clist[g, 1, o]]], axis=1)
                term = mm(lhs, coup[g, o])
                total = term if total is None else total + term
            far_acc[g] = total
            return 0

        lax.fori_loop(0, LEAVES, body, 0, unroll=2)

    copies["p"].wait_recv()
    couple([(0, 0, 1), (1, 0, 0), (0, -1, 0), (0, 1, 0)], True)

    copies["zp_fwd"].wait_recv()
    copies["zm_fwd"].wait_recv()
    send("z2_y", bufs[0, 2, 0], (1, 2, 0), whole, 1, 0, 0)
    send("z2_p", bufs[0, 2, 0], (0, 2, 1), whole, 0, 0, 1)

    relay(0)
    for name in ("y_p", "zp_p", "zm_p"):
        copies[name].wait_recv()
    couple([(1, 0, 1), (0, -1, 1), (0, 1, 1)], False)

    rc_load.wait()
    for c in ag:
        c.wait_recv()
    lhs = jnp.concatenate([vis[s].astype(bf16) for s in range(STEPS)], axis=1)
    rows = mm(lhs, rc[...])
    rf[l] = rows
    al = []
    for d in range(1, N_LEAF):
        c = pltpu.make_async_remote_copy(
            src_ref=rf.at[l], dst_ref=rf.at[l],
            send_sem=al_s.at[d - 1], recv_sem=al_r.at[d - 1], device_id={"leaf": (l + d) % N_LEAF},
        )
        c.start()
        al.append(c)

    relay(1)

    g = split(mm3(lt_h[...], lt_l[...], t_h[...], t_l[...]))
    g_h[...], g_l[...] = g

    copies["yzp"].wait_recv()
    send("yzp_p", bufs[1, -1, 0], (1, -1, 1), whole, 0, 0, 1)
    copies["yzm"].wait_recv()
    send("yzm_p", bufs[1, 1, 0], (1, 1, 1), whole, 0, 0, 1)

    nlist_load.wait()
    pl.when(has_down)(up.wait_recv)
    pl.when(has_up)(down.wait_recv)

    @pl.when(crosses)
    def _():
        for c in arrivals:
            c.wait_recv()

    base = (b * N_LEAF + l) * LEAVES - LEAVES

    def near_rest(g, _):
        lhs = jnp.concatenate([x[jnp.clip(nlist[g, k] - base, 0, 3 * LEAVES - 1)] for k in range(1, NEAR)], axis=1)
        prod[g] = prod[g] + mm(lhs, near_w[g, pl.ds(SIZE, (NEAR - 1) * SIZE), :])
        return 0

    lax.fori_loop(0, LEAVES, near_rest, 0, unroll=2)

    copies["z2_y"].wait_recv()
    send("yz2_p", bufs[1, 2, 0], (1, 2, 1), whole, 0, 0, 1)

    for name in ("z2_p", "yzp_p", "yzm_p"):
        copies[name].wait_recv()
    couple(
        [(1, -1, 0), (1, 1, 0), (0, 2, 0), (0, 2, 1), (1, -1, 1), (1, 1, 1), (1, 2, 0)], False
    )

    for c in al:
        c.wait_recv()
    r_h, r_l = split(rf[...].reshape(NRHS, RANK))
    down_leaf = mm3(r_h, r_l, g_h[...], g_l[...], mm_t)
    for g in range(LEAVES):
        far_acc[g] = far_acc[g] + down_leaf[:, g * RANK:(g + 1) * RANK]
    copies["yz2_p"].wait_recv()
    last = bufs[1, 2, 1]
    o = (b - blk_of(1, 2, 1) + N_BLK) % N_BLK - 1
    stores = []
    for g in range(LEAVES):
        lhs = jnp.concatenate([last[clist[g, 0, o]], last[clist[g, 1, o]]], axis=1)
        leaf_total = (far_acc[g] + mm(lhs, coup[g, o])).astype(bf16)
        prod[g] = prod[g] + mm_t(leaf_total, basis[g])
        c = pltpu.make_async_copy(prod.at[g], out.at[:, pl.ds(g * SIZE, SIZE)], osem.at[g])
        c.start()
        stores.append(c)

    for c in list(copies.values()) + rs + ag + al:
        c.wait_send()
    pl.when(has_up)(up.wait_send)
    pl.when(has_down)(down.wait_send)

    @pl.when(crosses)
    def _():
        for c in crossing:
            c.wait_send()

    @pl.when(relays)
    def _():
        for c in relayed:
            c.wait_send()

    for c in stores:
        c.wait()


def on_device(rhs, basis, near_list, near_block, local_transfer, cross_transfer, coupling_list, leaf_coupling, root_coupling):
    near_w = near_block.reshape(LEAVES, NEAR * SIZE, SIZE)
    coup = leaf_coupling.reshape(LEAVES, STEPS, SLOTS * RANK, RANK)
    rc = root_coupling.reshape(STEPS * RANK, RANK)
    V, S = pltpu.VMEM, pltpu.SemaphoreType
    dma = S.DMA
    scratch = [
        V((3 * LEAVES, NRHS, SIZE), bf16),
        V((LEAVES, SIZE, RANK), bf16),
        pltpu.SMEM((LEAVES, NEAR), jnp.int32),
        V((LEAVES, NEAR * SIZE, SIZE), bf16),
        V((LEAVES, RANK, RANK), f32),
        V((3, RANK, RANK), f32),
        pltpu.SMEM((LEAVES, SLOTS, STEPS), jnp.int32),
        V((LEAVES, STEPS, SLOTS * RANK, RANK), bf16),
        V((STEPS * RANK, RANK), bf16),
        V((LEAVES, NRHS, RANK), bf16),
        V((N_LEAF, ROWS, RANK), f32),
        V((N_LEAF - 1, ROWS, RANK), f32),
        V((ROWS, RANK), f32),
        V((STEPS, ROWS, RANK), f32),
        V((N_LEAF, ROWS, RANK), f32),
        V((LEAVES, NRHS, RANK), f32),
        V((LEAVES, NRHS, SIZE), f32),
        V((LEAVES * RANK, RANK), bf16),
        V((LEAVES * RANK, RANK), bf16),
        V((RANK, RANK), bf16),
        V((RANK, RANK), bf16),
        V((LEAVES * RANK, RANK), bf16),
        V((LEAVES * RANK, RANK), bf16),
    ]
    scratch += [V((LEAVES // 2, NRHS, SIZE), bf16), dma((6,)), dma((6,))]
    scratch += [V((LEAVES + 1, NRHS, RANK), bf16) for _ in SOURCES]
    scratch += [
        dma((32,)), dma((LEAVES,)), S.REGULAR, dma((2,)), dma((2,)), dma((17,)), dma((17,)),
        dma((7,)), dma((7,)), dma((15,)), dma((15,)), dma((7,)), dma((7,)),
    ]
    hbm = pl.BlockSpec(memory_space=pltpu.MemorySpace.HBM)
    return pl.pallas_call(
        kernel,
        out_shape=jax.ShapeDtypeStruct((NRHS, LEAVES * SIZE), f32),
        in_specs=[hbm] * 9,
        out_specs=hbm,
        scratch_shapes=scratch,
        compiler_params=pltpu.CompilerParams(
            collective_id=0, has_side_effects=True, vmem_limit_bytes=67043328
        ),
    )(rhs, basis, near_list, near_w, local_transfer, cross_transfer, coupling_list.transpose(0, 2, 1), coup, rc)


def solution(mesh):
    both = ("blk", "leaf")
    in_specs = (
        P(None, both), P(both, None, None), P(both, None), P(both, None, None, None), P(both, None, None),
        P("blk", None, None, None), P(both, None, None), P(both, None, None, None, None), P("blk", None, None, None),
    )
    return jax.shard_map(on_device, mesh=mesh, in_specs=in_specs, out_specs=P(None, both), check_vma=False)
```
